256 devices in a mesh: tok: 8 (over z), hid: 32 (over y, x, core).
Axes of the slice: x: 4, y: 4, z: 8, core: 2. Of those that a mesh axis runs over, the one named last changes fastest.
Arguments:
- out_grad: bfloat16 [2048, 8192], P('hid', 'tok'), may hold values from -6 to 6
- gate_act: bfloat16 [2048, 28672], P('tok', 'hid'), may hold values from -8 to 8
- up_act: bfloat16 [2048, 28672], P('tok', 'hid'), may hold values from -6 to 6
- gate_weight: bfloat16 [8192, 28672], P('tok', 'hid'), may hold values from -0.0625 to 0.0625
- up_weight: bfloat16 [8192, 28672], P('tok', 'hid'), may hold values from -0.0625 to 0.0625
- down_weight: bfloat16 [28672, 8192], P('hid', 'tok'), may hold values from -0.03125 to 0.03125
Outputs:
- input_grad: bfloat16 [2048, 8192], P('hid', 'tok')
The draws below stay inside these ranges and needn't reach their ends.
All inputs are finite; a program needn't handle non-finite values.
Results may differ from the reference program's by a relative error of at most 0.005.
Values may be sent and summed in bfloat16 or wider, within the bound.
No kernel may reach another device: no remote copies, remote signals or barrier semaphores. Data moves between devices by JAX's collectives and lax.ppermute only.
A program may use at most 64 MiB of HBM per device.

```python
import jax
import jax.numpy as jnp
from jax import lax

D = 8192
FF = 28672
TOKENS = 2048
N_HID = 32


def steps_of(own_key, shape, cuts, low, largest):
    factor_of, own = 1.0, jax.random.fold_in(own_key, 6)
    for axis_at, shards_of in cuts:
        draws = jnp.exp(jax.random.uniform(jax.random.fold_in(own, axis_at), (shards_of,), jnp.float32, low / len(cuts), largest / len(cuts)))
        factor_of = factor_of * jnp.repeat(draws, shape[axis_at] // shards_of).reshape([-1 if axis == axis_at else 1 for axis in range(len(shape))])
    return factor_of


def scatter_about(stream_key, extent, deviation, most, pieces=(), kind=jnp.bfloat16):
    drawn = jax.random.normal(stream_key, extent, jnp.float32) * deviation
    if len(pieces) > 0:
        drawn = steps_of(stream_key, extent, pieces, -0.22, 0.18) * drawn
    return jnp.clip(drawn, min=-most, max=most).astype(kind)


def setup_inputs(seed: int = 0) -> dict:
    splits = jax.random.split(jax.random.key(seed), 7)
    out_grad = scatter_about(splits[0], (TOKENS, D), 1.0, 6.0, ((0, 32), (1, 8)))
    gate_act = scatter_about(splits[1], (TOKENS, FF), 1.5, 8.0, ((0, 8), (1, 32)))
    up_act = scatter_about(splits[2], (TOKENS, FF), 1.0, 6.0, ((0, 8), (1, 32)))
    gate_weight = scatter_about(splits[3], (D, FF), D ** -0.5, 0.0625, ((0, 8), (1, 32)))
    up_weight = scatter_about(splits[4], (D, FF), D ** -0.5, 0.0625, ((0, 8), (1, 32)))
    down_weight = scatter_about(splits[5], (FF, D), FF ** -0.5, 0.03125, ((0, 32), (1, 8)))
    return {"out_grad": out_grad, "gate_act": gate_act, "up_act": up_act, "gate_weight": gate_weight, "up_weight": up_weight, "down_weight": down_weight}


def sylvester(order):
    index = jnp.arange(order, dtype=jnp.int32)
    anded = index[:, None] & index[None, :]
    count = jnp.zeros((order, order), jnp.int32)
    for level in range(order.bit_length()):
        count = count + ((anded >> level) & 1)
    return (1 - 2 * (count % 2)).astype(jnp.float32) * (1.0 / (order ** 0.5))


def reference(out_grad, gate_act, up_act, gate_weight, up_weight, down_weight):
    rotated_grad = lax.dot_general(out_grad, down_weight, (((1,), (1,)), ((), ())), preferred_element_type=jnp.float32)
    shaped = rotated_grad.reshape(TOKENS, N_HID, FF // N_HID)
    hadamard = sylvester(N_HID)
    hidden_grad = jnp.einsum("st,ktc->ksc", hadamard, shaped, precision=lax.Precision.HIGHEST).reshape(TOKENS, FF)
    gate = gate_act.astype(jnp.float32)
    upper = up_act.astype(jnp.float32)
    logistic = jax.nn.sigmoid(gate)
    gate_grad = (hidden_grad * upper * logistic * (1.0 + gate * (1.0 - logistic))).astype(jnp.bfloat16)
    up_grad = (hidden_grad * gate * logistic).astype(jnp.bfloat16)
    total = lax.dot_general(gate_grad, gate_weight, (((1,), (1,)), ((), ())), preferred_element_type=jnp.float32)
    total = total + lax.dot_general(up_grad, up_weight, (((1,), (1,)), ((), ())), preferred_element_type=jnp.float32)
    return total.astype(jnp.bfloat16)
```

```python
import math

import jax
import jax.numpy as jnp
from jax import lax
from jax.experimental import pallas as pl
from jax.experimental.pallas import tpu as pltpu
from jax.sharding import Mesh
from jax.sharding import PartitionSpec as P


HID = ("y", "x", "core")
NY, NX, NC, NZ = 4, 4, 2, 8
BF, F32 = jnp.bfloat16, jnp.float32


def hid_index(y, x, c):
    return ((y % NY) * NX + x % NX) * NC + c


def plane_shift(value, first, amount):
    pairs = []
    for y in range(NY):
        for x in range(NX):
            for c in range(NC):
                along_x = (c == 0) == first
                target = hid_index(y, x + amount, c) if along_x else hid_index(y + amount, x, c)
                pairs.append((hid_index(y, x, c), target))
    return lax.ppermute(value, HID, pairs)


def core_swap(value):
    return lax.ppermute(value, "core", [(0, 1), (1, 0)])


def ring(value, step):
    return lax.ppermute(value, "tok", [(i, (i + step) % NZ) for i in range(NZ)])


def contract_rows(left, right):
    return lax.dot_general(left, right, (((1,), (1,)), ((), ())), preferred_element_type=F32)


def pinned(value):
    return lax.optimization_barrier(value)


def put(buffer, block, index):
    return lax.dynamic_update_slice_in_dim(buffer, block[None], index, 0)


def gather_tokens(out_grad, y, x, c):
    f = jnp.where(c == 0, x, y)
    s = jnp.where(c == 0, y, x)

    def stage(block, first, position):
        buffer = jnp.zeros((4, *block.shape), block.dtype)
        far = plane_shift(block, first, 2)
        up = plane_shift(block, first, 1)
        down = plane_shift(block, first, -1)
        buffer = put(buffer, block, position)
        buffer = put(buffer, far, (position + 2) % 4)
        buffer = put(buffer, up, (position + 3) % 4)
        return put(buffer, down, (position + 1) % 4)

    both = stage(stage(out_grad, True, f), False, s)
    own = jnp.where(c == 0, both, jnp.swapaxes(both, 0, 1))
    own = pinned(own.reshape(16, *out_grad.shape))
    return own, core_swap(own)


def hadamard_kernel(in_ref, out_ref):
    count = in_ref.shape[0]
    scale = 1.0 / math.sqrt(count)

    def columns(i, carry):
        at = pl.ds(pl.multiple_of(i * 128, 128), 128)
        rows = [in_ref[t, :, at] for t in range(count)]
        level = 1
        while level < count:
            rows = [
                rows[t] + rows[t | level] if not t & level else rows[t ^ level] - rows[t]
                for t in range(count)
            ]
            level *= 2
        for t in range(count):
            out_ref[t, :, at] = rows[t] * scale
        return carry

    lax.fori_loop(0, in_ref.shape[2] // 128, columns, 0)


def hadamard(values):
    return pl.pallas_call(
        hadamard_kernel,
        out_shape=jax.ShapeDtypeStruct(values.shape, F32),
        in_specs=[pl.BlockSpec(memory_space=pltpu.VMEM)],
        out_specs=pl.BlockSpec(memory_space=pltpu.VMEM),
        cost_estimate=pl.CostEstimate(flops=5 * values.size, bytes_accessed=8 * values.size, transcendentals=0),
    )(values)


def gates_kernel(hidden_ref, gate_ref, up_ref, low_ref, high_ref):
    for part, out_ref in enumerate((low_ref, high_ref)):
        for block in range(4):
            source = pl.ds(block * 64 + part * 32, 32)
            target = pl.ds(block * 32, 32)
            hidden = hidden_ref[source, :]
            gate = gate_ref[source, :].astype(F32)
            upper = up_ref[source, :].astype(F32)
            logistic = 1.0 / (1.0 + jnp.exp(-gate))
            out_ref[0, target, :] = (hidden * upper * logistic * (1.0 + gate * (1.0 - logistic))).astype(BF)
            out_ref[1, target, :] = (hidden * gate * logistic).astype(BF)


def gates(hidden, gate, upper):
    rows, columns = hidden.shape
    shape = jax.ShapeDtypeStruct((2, rows // 2, columns), BF)
    return pl.pallas_call(
        gates_kernel,
        out_shape=(shape, shape),
        in_specs=[pl.BlockSpec(memory_space=pltpu.VMEM)] * 3,
        out_specs=(pl.BlockSpec(memory_space=pltpu.VMEM),) * 2,
        cost_estimate=pl.CostEstimate(flops=12 * hidden.size, bytes_accessed=12 * hidden.size, transcendentals=hidden.size),
    )(hidden, gate, upper)


def body(out_grad, gate_act, up_act, gate_weight, up_weight, down_weight):
    z, y, x, c = (lax.axis_index(name) for name in ("tok", "y", "x", "core"))
    own, other = gather_tokens(out_grad, y, x, c)
    width = out_grad.shape[1]

    def partial(offset):
        at = 2 * ((z + offset) % NZ)
        mine = lax.dynamic_slice_in_dim(own, at, 2, 0)
        theirs = lax.dynamic_slice_in_dim(other, at, 2, 0)
        rows = jnp.stack([mine, theirs], axis=1).reshape(256, width)
        return pinned(contract_rows(rows, down_weight))

    order = (4, 3, 5, 2, 6, 1, 7, 0)
    partials = {offset: partial(offset) for offset in order}

    def chain(part, direction):
        def rows(offset):
            return partials[offset % NZ][part * 128 : part * 128 + 128]

        if direction == 1:
            arrived = ring(rows(4)[:64].astype(BF), 1).astype(F32)
            total = jnp.concatenate([rows(3)[:64] + arrived, rows(3)[64:]], axis=0)
        else:
            arrived = ring(rows(4)[64:].astype(BF), -1).astype(F32)
            total = jnp.concatenate([rows(-3)[:64], rows(-3)[64:] + arrived], axis=0)
        for offset in (2, 1):
            total = rows(direction * offset) + ring(total.astype(BF), direction).astype(F32)
        return ring(total.astype(BF), direction).astype(F32)

    arrived = [(chain(part, 1), chain(part, -1)) for part in range(2)]
    rotated = partials[0] + jnp.concatenate([a + b for a, b in arrived], axis=0)
    rotated = rotated.reshape(2, 2, 64, -1)
    rotated = jnp.where(c == 0, rotated, rotated[:, ::-1])

    mixed = lax.all_to_all(rotated.reshape(32, 8, -1), HID, 0, 0)
    hidden = lax.all_to_all(hadamard(mixed), HID, 0, 0).reshape(256, -1)

    parts = gates(hidden, gate_act, up_act)

    def back(gate, upper):
        return contract_rows(gate, gate_weight) + contract_rows(upper, up_weight)

    result = jnp.zeros((NZ, 4, 2, 32, width), F32)

    def place(result, rows, offset, part):
        block = rows.reshape(1, 4, 1, 32, width)
        return lax.dynamic_update_slice(result, block, ((z + offset) % NZ, 0, part, 0, 0))

    both = back(*(jnp.concatenate([parts[0][i], parts[1][i]], axis=0) for i in range(2)))
    result = place(place(result, both[:128], 0, 0), both[128:], 0, 1)
    right, left = list(parts), list(parts)
    for step in (1, 2, 3):
        for part in range(2):
            right[part], left[part] = ring(right[part], 1), ring(left[part], -1)
        for part in range(2):
            rows = back(*(jnp.concatenate([right[part][i], left[part][i]], axis=0) for i in range(2)))
            result = place(place(result, rows[:128], -step, part), rows[128:], step, part)
    for part in range(2):
        rows = back(ring(right[part][0], 1), ring(left[part][1], -1))
        result = place(result, rows, 4, part)

    result = result.reshape(16, 2, 64, width)
    keep = lax.dynamic_index_in_dim(result, c, 1, keepdims=False)
    send = lax.dynamic_index_in_dim(result, 1 - c, 1, keepdims=False).astype(BF)
    summed = (keep + core_swap(send).astype(F32)).astype(BF)
    pieces = lax.all_to_all(summed, ("y", "x"), 0, 0)
    return jnp.sum(pieces.astype(F32), axis=0).astype(BF)


def solution(mesh):
    fine = Mesh(mesh.devices.reshape(NZ, NY, NX, NC), ("tok", *HID))
    rows, columns = P(HID, "tok"), P("tok", HID)
    in_specs = (rows, columns, columns, columns, columns, rows)
    return jax.shard_map(body, mesh=fine, in_specs=in_specs, out_specs=rows, check_vma=False)
```

```python
import math

import jax
import jax.numpy as jnp
from jax import lax
from jax.experimental import pallas as pl
from jax.experimental.pallas import tpu as pltpu
from jax.sharding import Mesh
from jax.sharding import PartitionSpec as P


HID = ("y", "x", "core")
NY, NX, NC, NZ = 4, 4, 2, 8
BF, F32 = jnp.bfloat16, jnp.float32


def hid_index(y, x, c):
    return ((y % NY) * NX + x % NX) * NC + c


def plane_shift(value, first, amount):
    pairs = []
    for y in range(NY):
        for x in range(NX):
            for c in range(NC):
                along_x = (c == 0) == first
                target = hid_index(y, x + amount, c) if along_x else hid_index(y + amount, x, c)
                pairs.append((hid_index(y, x, c), target))
    return lax.ppermute(value, HID, pairs)


def core_swap(value):
    return lax.ppermute(value, "core", [(0, 1), (1, 0)])


def ring(value, step):
    return lax.ppermute(value, "tok", [(i, (i + step) % NZ) for i in range(NZ)])


def contract_rows(left, right):
    return lax.dot_general(left, right, (((1,), (1,)), ((), ())), preferred_element_type=F32)


class Place:
    def __init__(self):
        self.z, self.y, self.x, self.c = (lax.axis_index(name) for name in ("tok", *HID))
        self.first = jnp.where(self.c == 0, self.x, self.y)
        self.second = jnp.where(self.c == 0, self.y, self.x)

    def block(self, first, second):
        first, second = first % 4, second % 4
        y = jnp.where(self.c == 0, second, first)
        x = jnp.where(self.c == 0, first, second)
        return ((2 * y + x // 2 - self.z) % NZ) * 2 + x % 2


FROM = (0, 2, -1, 1)


def spread(block, first):
    return [block] + [plane_shift(block, first, amount) for amount in (2, 1, -1)]


def gather_tokens(out_grad, place):
    stack = jnp.stack(spread(out_grad, True))
    own = jnp.zeros((16, *out_grad.shape), BF)
    for second, piece in zip(FROM, spread(stack, False)):
        for k, first in enumerate(FROM):
            at = place.block(place.first + first, place.second + second)
            own = lax.dynamic_update_slice_in_dim(own, piece[k : k + 1], at, 0)
    return own


def hadamard_kernel(in_ref, out_ref):
    count, rows, columns = in_ref.shape
    scale = 1.0 / math.sqrt(2 * count)
    tiles = columns // 128

    def tile(i, carry):
        down = pl.ds(pl.multiple_of(i // tiles * 8, 8), 8)
        across = pl.ds(pl.multiple_of(i % tiles * 128, 128), 128)
        values = [in_ref[t, down, across] for t in range(count)]
        level = 1
        while level < count:
            values = [
                values[t] + values[t | level] if not t & level else values[t ^ level] - values[t]
                for t in range(count)
            ]
            level *= 2
        for t in range(count):
            out_ref[t, down, across] = values[t] * scale
        return carry

    lax.fori_loop(0, rows // 8 * tiles, tile, 0)


def hadamard(values):
    return pl.pallas_call(
        hadamard_kernel,
        out_shape=jax.ShapeDtypeStruct(values.shape, F32),
        in_specs=[pl.BlockSpec(memory_space=pltpu.VMEM)],
        out_specs=pl.BlockSpec(memory_space=pltpu.VMEM),
        cost_estimate=pl.CostEstimate(flops=5 * values.size, bytes_accessed=8 * values.size, transcendentals=0),
    )(values)


def gates_kernel(core_ref, mixed_ref, other_ref, gate_ref, up_ref, low_ref, high_ref):
    core = core_ref[0]
    for part, out_ref in enumerate((low_ref, high_ref)):
        for side in range(2):
            for low in range(2):
                groups = pl.ds(low * 8 + part * 4, 4)
                hidden = mixed_ref[groups, 0] if side == 0 else other_ref[groups]
                hidden = hidden.reshape(32, -1)
                which = core if side == 0 else 1 - core
                source = pl.ds(pl.multiple_of(low * 128 + which * 64 + part * 32, 32), 32)
                target = pl.ds(side * 64 + low * 32, 32)
                gate = gate_ref[source, :].astype(F32)
                upper = up_ref[source, :].astype(F32)
                logistic = 1.0 / (1.0 + jnp.exp(-gate))
                out_ref[0, target, :] = (hidden * upper * logistic * (1.0 + gate * (1.0 - logistic))).astype(BF)
                out_ref[1, target, :] = (hidden * gate * logistic).astype(BF)


def gates(core, mixed, other, gate, upper):
    rows, columns = gate.shape
    shape = jax.ShapeDtypeStruct((2, rows // 2, columns), BF)
    return pl.pallas_call(
        gates_kernel,
        out_shape=(shape, shape),
        in_specs=[pl.BlockSpec(memory_space=pltpu.SMEM)] + [pl.BlockSpec(memory_space=pltpu.VMEM)] * 4,
        out_specs=(pl.BlockSpec(memory_space=pltpu.VMEM),) * 2,
        cost_estimate=pl.CostEstimate(flops=12 * gate.size, bytes_accessed=12 * gate.size, transcendentals=gate.size),
    )(core.reshape(1), mixed, other, gate, upper)


def scatter_sum(partials):
    def chain(direction):
        def rows(offset):
            return partials[direction * offset % NZ]

        def hop(total):
            return ring(total.astype(BF), direction).astype(F32)

        near = slice(0, 64) if direction == 1 else slice(64, 128)
        parts = [rows(3)[:64], rows(3)[64:]]
        arrived = hop(rows(4)[near])
        parts[0 if direction == 1 else 1] += arrived
        total = jnp.concatenate(parts, axis=0)
        for offset in (2, 1):
            total = rows(offset) + hop(total)
        return hop(total)

    return partials[0] + chain(1) + chain(-1)


def mix(own, other, place):
    theirs = core_swap(other)
    total = own + theirs
    difference = jnp.where(place.c == 0, own - theirs, theirs - own)
    difference, total = (
        jnp.where(place.c == 0, difference, total),
        jnp.where(place.c == 0, total, difference),
    )
    rows = jnp.stack([total.reshape(16, 8, -1), difference.reshape(16, 8, -1)], axis=1)
    there = lax.all_to_all(rows.reshape(16, 16, -1), ("y", "x"), 0, 0)
    back = lax.all_to_all(hadamard(there), ("y", "x"), 0, 0).reshape(rows.shape)
    return back, core_swap(back[:, 1])


def step(out_grad, gate_act, up_act, gate_weight, up_weight, down_weight):
    place = Place()
    width = out_grad.shape[1]
    tokens = gather_tokens(out_grad, place)
    other_tokens = core_swap(tokens)

    def partials(rows):
        return contract_rows(rows.reshape(-1, width), down_weight).reshape(NZ, 128, -1)

    own = scatter_sum(partials(tokens))
    other = scatter_sum(partials(other_tokens))
    mixed, other_hidden = mix(own, other, place)
    parts = gates(place.c, mixed, other_hidden, gate_act, up_act)

    def back(gate, upper):
        rows = contract_rows(gate, gate_weight) + contract_rows(upper, up_weight)
        return rows.reshape(-1, 2, 64, width)

    def finish(part):
        right = left = part
        keep = jnp.zeros((NZ, 64, width), F32)
        send = jnp.zeros((NZ, 64, width), BF)

        def store(rows, *offsets):
            nonlocal keep, send
            for i, offset in enumerate(offsets):
                at = offset % NZ
                keep = keep.at[at].set(rows[i, 0])
                send = send.at[at].set(rows[i, 1].astype(BF))

        rows = back(part[0], part[1])
        store(rows, 0)
        for step in (1, 2, 3):
            right = ring(right, 1)
            left = ring(left, -1)
            rows = back(*(jnp.concatenate([right[i], left[i]], axis=0) for i in range(2)))
            store(rows, -step, step)
        right = ring(right[0], 1)
        left = ring(left[1], -1)
        rows = back(right, left)
        store(rows, 4)
        keep = keep.reshape(16, 32, width)
        arrived = core_swap(send).reshape(16, 32, width)

        def message(distance):
            def at(k):
                index = place.block(place.first + distance, jnp.int32(k))
                return (
                    lax.dynamic_slice_in_dim(keep, index, 1, 0)
                    + lax.dynamic_slice_in_dim(arrived, index, 1, 0).astype(F32)
                )

            return jnp.concatenate([at(k) for k in range(4)], axis=0)

        total = message(0)
        for distance in (2, 1, -1):
            total += plane_shift(message(distance).astype(BF), True, distance).astype(F32)

        def row(distance):
            return lax.dynamic_index_in_dim(total, (place.second + distance) % 4, 0, keepdims=False)

        result = row(0)
        for distance in (2, 1, -1):
            result += plane_shift(row(distance).astype(BF), False, distance).astype(F32)
        return result.astype(BF)

    return jnp.concatenate([finish(part) for part in parts], axis=0)


def solution(mesh):
    fine = Mesh(mesh.devices.reshape(NZ, NY, NX, NC), ("tok", *HID))
    rows, columns = P(HID, "tok"), P("tok", HID)
    in_specs = (rows, columns, columns, columns, columns, rows)
    return jax.shard_map(step, mesh=fine, in_specs=in_specs, out_specs=rows, check_vma=False)
```

```python
import math

import jax
import jax.numpy as jnp
from jax import lax
from jax.experimental import pallas as pl
from jax.experimental.pallas import tpu as pltpu
from jax.sharding import Mesh
from jax.sharding import PartitionSpec as P


HID = ("y", "x", "core")
NY, NX, NC, NZ = 4, 4, 2, 8
BF, F32 = jnp.bfloat16, jnp.float32


def hid_index(y, x, c):
    return ((y % NY) * NX + x % NX) * NC + c


def plane_shift(value, first, amount):
    pairs = []
    for y in range(NY):
        for x in range(NX):
            for c in range(NC):
                along_x = (c == 0) == first
                target = hid_index(y, x + amount, c) if along_x else hid_index(y + amount, x, c)
                pairs.append((hid_index(y, x, c), target))
    return lax.ppermute(value, HID, pairs)


def core_swap(value):
    return lax.ppermute(value, "core", [(0, 1), (1, 0)])


def ring(value, step):
    return lax.ppermute(value, "tok", [(i, (i + step) % NZ) for i in range(NZ)])


def contract_rows(left, right):
    return lax.dot_general(left, right, (((1,), (1,)), ((), ())), preferred_element_type=F32)


class Place:
    def __init__(self):
        self.z, self.y, self.x, self.c = (lax.axis_index(name) for name in ("tok", *HID))
        self.first = jnp.where(self.c == 0, self.x, self.y)
        self.second = jnp.where(self.c == 0, self.y, self.x)

    def block(self, first, second):
        first, second = first % 4, second % 4
        y = jnp.where(self.c == 0, second, first)
        x = jnp.where(self.c == 0, first, second)
        return ((2 * y + x // 2 - self.z) % NZ) * 2 + x % 2


FROM = (0, 2, -1, 1)


def spread(block, first):
    return [block] + [plane_shift(block, first, amount) for amount in (2, 1, -1)]


def gather_tokens(out_grad, place):
    stack = jnp.stack(spread(out_grad, True))
    own = jnp.zeros((16, *out_grad.shape), BF)
    for second, piece in zip(FROM, spread(stack, False)):
        for k, first in enumerate(FROM):
            at = place.block(place.first + first, place.second + second)
            own = lax.dynamic_update_slice_in_dim(own, piece[k : k + 1], at, 0)
    return own


def hadamard_kernel(in_ref, out_ref):
    count, rows, columns = in_ref.shape
    scale = 1.0 / math.sqrt(2 * count)
    tiles = columns // 128

    def tile(i, carry):
        down = pl.ds(pl.multiple_of(i // tiles * 8, 8), 8)
        across = pl.ds(pl.multiple_of(i % tiles * 128, 128), 128)
        values = [in_ref[t, down, across] for t in range(count)]
        level = 1
        while level < count:
            values = [
                values[t] + values[t | level] if not t & level else values[t ^ level] - values[t]
                for t in range(count)
            ]
            level *= 2
        for t in range(count):
            out_ref[t, down, across] = values[t] * scale
        return carry

    lax.fori_loop(0, rows // 8 * tiles, tile, 0)


def hadamard(values):
    return pl.pallas_call(
        hadamard_kernel,
        out_shape=jax.ShapeDtypeStruct(values.shape, F32),
        in_specs=[pl.BlockSpec(memory_space=pltpu.VMEM)],
        out_specs=pl.BlockSpec(memory_space=pltpu.VMEM),
        cost_estimate=pl.CostEstimate(flops=5 * values.size, bytes_accessed=8 * values.size, transcendentals=0),
    )(values)


def gates_kernel(core_ref, hidden_ref, gate_ref, up_ref, out_ref):
    half = hidden_ref.shape[0] // 2
    for low in range(2):
        hidden = hidden_ref[pl.ds(low * half, half)].reshape(64, -1)
        source = pl.ds(pl.multiple_of(low * 128 + core_ref[0] * 64, 64), 64)
        target = pl.ds(low * 64, 64)
        gate = gate_ref[source, :].astype(F32)
        upper = up_ref[source, :].astype(F32)
        logistic = 1.0 / (1.0 + jnp.exp(-gate))
        out_ref[0, target, :] = (hidden * upper * logistic * (1.0 + gate * (1.0 - logistic))).astype(BF)
        out_ref[1, target, :] = (hidden * gate * logistic).astype(BF)


def gates(core, hidden, gate, upper):
    size = hidden.size
    return pl.pallas_call(
        gates_kernel,
        out_shape=jax.ShapeDtypeStruct((2, 128, hidden.shape[-1]), BF),
        in_specs=[pl.BlockSpec(memory_space=pltpu.SMEM)] + [pl.BlockSpec(memory_space=pltpu.VMEM)] * 3,
        out_specs=pl.BlockSpec(memory_space=pltpu.VMEM),
        cost_estimate=pl.CostEstimate(flops=12 * size, bytes_accessed=12 * size, transcendentals=size),
    )(core.reshape(1), hidden, gate, upper)


def scatter_sum(own, other):
    def chain(direction):
        def rows(offset):
            return [side[direction * offset % NZ] for side in (own, other)]

        def hop(total):
            return ring(total.astype(BF), direction).astype(F32)

        side = 0 if direction == 1 else 1
        parts = rows(3)
        parts[side] = parts[side] + hop(rows(4)[side])
        total = jnp.stack(parts)
        for offset in (2, 1):
            total = jnp.stack(rows(offset)) + hop(total)
        return hop(total)

    right, left = chain(1), chain(-1)
    return own[0] + right[0] + left[0], other[0] + right[1] + left[1]


def mix(own, other, place):
    theirs = core_swap(other)
    total = own + theirs
    difference = jnp.where(place.c == 0, own - theirs, theirs - own)
    difference, total = (
        jnp.where(place.c == 0, difference, total),
        jnp.where(place.c == 0, total, difference),
    )
    rows = jnp.stack([total.reshape(16, 8, -1), difference.reshape(16, 8, -1)], axis=1)
    there = lax.all_to_all(rows.reshape(16, 16, -1), ("y", "x"), 0, 0)
    back = lax.all_to_all(hadamard(there), ("y", "x"), 0, 0).reshape(rows.shape)
    return back[:, 0], core_swap(back[:, 1])


def step(out_grad, gate_act, up_act, gate_weight, up_weight, down_weight):
    place = Place()
    width = out_grad.shape[1]
    tokens = gather_tokens(out_grad, place)
    other_tokens = core_swap(tokens)

    def partials(rows):
        return contract_rows(rows.reshape(-1, width), down_weight).reshape(NZ, 128, -1)

    own, other = scatter_sum(partials(tokens), partials(other_tokens))
    own, other = mix(own, other, place)
    own = gates(place.c, own, gate_act, up_act)
    other = gates(1 - place.c, other, gate_act, up_act)

    def back(part, dtype):
        right = left = part
        result = lax.optimization_barrier(jnp.zeros((NZ, 128, width), dtype))

        def product(gate, upper):
            rows = contract_rows(gate, gate_weight) + contract_rows(upper, up_weight)
            return rows.astype(dtype)

        def move(way, value):
            return ring(value, 1 if way == "r" else -1)

        result = result.at[0].set(product(part[0], part[1]))
        for step in (1, 2, 3):
            right, left = move("r", right), move("l", left)
            pair = [jnp.concatenate([right[i], left[i]], axis=0) for i in range(2)]
            rows = product(*pair)
            result = result.at[NZ - step].set(rows[:128]).at[step].set(rows[128:])
        return result.at[4].set(product(move("r", right[0]), move("l", left[1])))

    arrived = core_swap(back(other, BF)).reshape(16, 64, width)
    keep = back(own, F32).reshape(16, 64, width)

    def message(distance):
        def at(k):
            index = place.block(place.first + distance, jnp.int32(k))
            return (
                lax.dynamic_slice_in_dim(keep, index, 1, 0)
                + lax.dynamic_slice_in_dim(arrived, index, 1, 0).astype(F32)
            )

        return jnp.concatenate([at(k) for k in range(4)], axis=0)

    total = message(0)
    for distance in (2, 1, -1):
        total += plane_shift(message(distance).astype(BF), True, distance).astype(F32)

    def row(distance):
        return lax.dynamic_index_in_dim(total, (place.second + distance) % 4, 0, keepdims=False)

    result = row(0)
    for distance in (2, 1, -1):
        result += plane_shift(row(distance).astype(BF), False, distance).astype(F32)
    return result.astype(BF)


def solution(mesh):
    fine = Mesh(mesh.devices.reshape(NZ, NY, NX, NC), ("tok", *HID))
    rows, columns = P(HID, "tok"), P("tok", HID)
    in_specs = (rows, columns, columns, columns, columns, rows)
    return jax.shard_map(step, mesh=fine, in_specs=in_specs, out_specs=rows, check_vma=False)
```

```python
import math

import jax
import jax.numpy as jnp
from jax import lax
from jax.experimental import pallas as pl
from jax.experimental.pallas import tpu as pltpu
from jax.sharding import Mesh
from jax.sharding import PartitionSpec as P


HID = ("y", "x", "core")
NY, NX, NC, NZ = 4, 4, 2, 8
BF, F32 = jnp.bfloat16, jnp.float32


def hid_index(y, x, c):
    return ((y % NY) * NX + x % NX) * NC + c


def plane_shift(value, first, amount):
    pairs = []
    for y in range(NY):
        for x in range(NX):
            for c in range(NC):
                along_x = (c == 0) == first
                target = hid_index(y, x + amount, c) if along_x else hid_index(y + amount, x, c)
                pairs.append((hid_index(y, x, c), target))
    return lax.ppermute(value, HID, pairs)


def core_swap(value):
    return lax.ppermute(value, "core", [(0, 1), (1, 0)])


def ring(value, step):
    return lax.ppermute(value, "tok", [(i, (i + step) % NZ) for i in range(NZ)])


def contract_rows(left, right):
    return lax.dot_general(left, right, (((1,), (1,)), ((), ())), preferred_element_type=F32)


class Place:
    def __init__(self):
        self.z, self.y, self.x, self.c = (lax.axis_index(name) for name in ("tok", *HID))
        self.first = jnp.where(self.c == 0, self.x, self.y)
        self.second = jnp.where(self.c == 0, self.y, self.x)

    def block(self, first, second):
        first, second = first % 4, second % 4
        y = jnp.where(self.c == 0, second, first)
        x = jnp.where(self.c == 0, first, second)
        return ((2 * y + x // 2 - self.z) % NZ) * 2 + x % 2


FROM = (0, 2, -1, 1)


def spread(block, first):
    return [block] + [plane_shift(block, first, amount) for amount in (2, 1, -1)]


def gather_tokens(out_grad, place):
    stack = jnp.stack(spread(out_grad, True))
    own = jnp.zeros((16, *out_grad.shape), BF)
    for second, piece in zip(FROM, spread(stack, False)):
        for k, first in enumerate(FROM):
            at = place.block(place.first + first, place.second + second)
            own = lax.dynamic_update_slice_in_dim(own, piece[k : k + 1], at, 0)
    return own


def hadamard_kernel(in_ref, out_ref):
    count, rows, columns = in_ref.shape
    scale = 1.0 / math.sqrt(2 * count)
    tiles = columns // 128

    def tile(i, carry):
        down = pl.ds(pl.multiple_of(i // tiles * 8, 8), 8)
        across = pl.ds(pl.multiple_of(i % tiles * 128, 128), 128)
        values = [in_ref[t, down, across] for t in range(count)]
        level = 1
        while level < count:
            values = [
                values[t] + values[t | level] if not t & level else values[t ^ level] - values[t]
                for t in range(count)
            ]
            level *= 2
        for t in range(count):
            out_ref[t, down, across] = values[t] * scale
        return carry

    lax.fori_loop(0, rows // 8 * tiles, tile, 0)


def hadamard(values):
    return pl.pallas_call(
        hadamard_kernel,
        out_shape=jax.ShapeDtypeStruct(values.shape, F32),
        in_specs=[pl.BlockSpec(memory_space=pltpu.VMEM)],
        out_specs=pl.BlockSpec(memory_space=pltpu.VMEM),
        cost_estimate=pl.CostEstimate(flops=5 * values.size, bytes_accessed=8 * values.size, transcendentals=0),
    )(values)


def gates_kernel(core_ref, hidden_ref, gate_ref, up_ref, out_ref):
    half = hidden_ref.shape[0] // 2
    for low in range(2):
        hidden = hidden_ref[pl.ds(low * half, half)].reshape(64, -1)
        source = pl.ds(pl.multiple_of(low * 128 + core_ref[0] * 64, 64), 64)
        target = pl.ds(low * 64, 64)
        gate = gate_ref[source, :].astype(F32)
        upper = up_ref[source, :].astype(F32)
        logistic = 1.0 / (1.0 + jnp.exp(-gate))
        out_ref[0, target, :] = (hidden * upper * logistic * (1.0 + gate * (1.0 - logistic))).astype(BF)
        out_ref[1, target, :] = (hidden * gate * logistic).astype(BF)


def gates(core, hidden, gate, upper):
    size = hidden.size
    return pl.pallas_call(
        gates_kernel,
        out_shape=jax.ShapeDtypeStruct((2, 128, hidden.shape[-1]), BF),
        in_specs=[pl.BlockSpec(memory_space=pltpu.SMEM)] + [pl.BlockSpec(memory_space=pltpu.VMEM)] * 3,
        out_specs=pl.BlockSpec(memory_space=pltpu.VMEM),
        cost_estimate=pl.CostEstimate(flops=12 * size, bytes_accessed=12 * size, transcendentals=size),
    )(core.reshape(1), hidden, gate, upper)


def scatter_sum(own, other):
    def chain(direction):
        def rows(offset):
            return [side[direction * offset % NZ] for side in (own, other)]

        def hop(total):
            return ring(total.astype(BF), direction).astype(F32)

        side = 0 if direction == 1 else 1
        parts = rows(3)
        parts[side] = parts[side] + hop(rows(4)[side])
        total = jnp.stack(parts)
        for offset in (2, 1):
            total = jnp.stack(rows(offset)) + hop(total)
        return hop(total)

    right, left = chain(1), chain(-1)
    return own[0] + right[0] + left[0], other[0] + right[1] + left[1]


def mix(own, other, place):
    theirs = core_swap(other)
    total = own + theirs
    difference = jnp.where(place.c == 0, own - theirs, theirs - own)
    difference, total = (
        jnp.where(place.c == 0, difference, total),
        jnp.where(place.c == 0, total, difference),
    )
    rows = jnp.stack([total.reshape(16, 8, -1), difference.reshape(16, 8, -1)], axis=1)
    there = lax.all_to_all(rows.reshape(16, 16, -1), ("y", "x"), 0, 0)
    back = lax.all_to_all(hadamard(there), ("y", "x"), 0, 0).reshape(rows.shape)
    return back[:, 0], core_swap(back[:, 1])


def step(out_grad, gate_act, up_act, gate_weight, up_weight, down_weight):
    place = Place()
    width = out_grad.shape[1]
    tokens = gather_tokens(out_grad, place)
    other_tokens = core_swap(tokens)

    def partials(rows):
        return contract_rows(rows.reshape(-1, width), down_weight).reshape(NZ, 128, -1)

    own, other = scatter_sum(partials(tokens), partials(other_tokens))
    own, other = mix(own, other, place)
    own = gates(place.c, own, gate_act, up_act)
    other = gates(1 - place.c, other, gate_act, up_act)

    def back(part, dtype):
        right = left = part
        result = lax.optimization_barrier(jnp.zeros((NZ, 128, width), dtype))

        def product(gate, upper):
            rows = contract_rows(gate, gate_weight) + contract_rows(upper, up_weight)
            return rows.astype(dtype)

        def move(way, value):
            return ring(value, 1 if way == "r" else -1)

        result = result.at[0].set(product(part[0], part[1]))
        for step in (1, 2, 3):
            right, left = move("r", right), move("l", left)
            pair = [jnp.concatenate([right[i], left[i]], axis=0) for i in range(2)]
            rows = product(*pair)
            result = result.at[NZ - step].set(rows[:128]).at[step].set(rows[128:])
        return result, product(move("r", right[0]), move("l", left[1]))

    early, last = back(other, BF)
    early = core_swap(early)
    last = core_swap(last)
    arrived = early.at[4].set(last).reshape(16, 64, width)
    keep, last = back(own, F32)
    keep = keep.at[4].set(last).reshape(16, 64, width)

    def message(distance):
        def at(k):
            index = place.block(place.first + distance, jnp.int32(k))
            return (
                lax.dynamic_slice_in_dim(keep, index, 1, 0)
                + lax.dynamic_slice_in_dim(arrived, index, 1, 0).astype(F32)
            )

        return jnp.concatenate([at(k) for k in range(4)], axis=0)

    total = message(0)
    for distance in (2, 1, -1):
        total += plane_shift(message(distance).astype(BF), True, distance).astype(F32)

    def row(distance):
        return lax.dynamic_index_in_dim(total, (place.second + distance) % 4, 0, keepdims=False)

    result = row(0)
    for distance in (2, 1, -1):
        result += plane_shift(row(distance).astype(BF), False, distance).astype(F32)
    return result.astype(BF)


def solution(mesh):
    fine = Mesh(mesh.devices.reshape(NZ, NY, NX, NC), ("tok", *HID))
    rows, columns = P(HID, "tok"), P("tok", HID)
    in_specs = (rows, columns, columns, columns, columns, rows)
    return jax.shard_map(step, mesh=fine, in_specs=in_specs, out_specs=rows, check_vma=False)
```

```python
import math

import jax
import jax.numpy as jnp
from jax import lax
from jax.experimental import pallas as pl
from jax.experimental.pallas import tpu as pltpu
from jax.sharding import Mesh
from jax.sharding import PartitionSpec as P


HID = ("y", "x", "core")
NY, NX, NC, NZ = 4, 4, 2, 8
BF, F32 = jnp.bfloat16, jnp.float32


def hid_index(y, x, c):
    return ((y % NY) * NX + x % NX) * NC + c


def plane_shift(value, first, amount):
    pairs = []
    for y in range(NY):
        for x in range(NX):
            for c in range(NC):
                along_x = (c == 0) == first
                target = hid_index(y, x + amount, c) if along_x else hid_index(y + amount, x, c)
                pairs.append((hid_index(y, x, c), target))
    return lax.ppermute(value, HID, pairs)


def core_swap(value):
    return lax.ppermute(value, "core", [(0, 1), (1, 0)])


def ring(value, step):
    return lax.ppermute(value, "tok", [(i, (i + step) % NZ) for i in range(NZ)])


def contract_rows(left, right):
    return lax.dot_general(left, right, (((1,), (1,)), ((), ())), preferred_element_type=F32)


class Place:
    def __init__(self):
        self.z, self.y, self.x, self.c = (lax.axis_index(name) for name in ("tok", *HID))
        self.first = jnp.where(self.c == 0, self.x, self.y)
        self.second = jnp.where(self.c == 0, self.y, self.x)

    def block(self, first, second):
        first, second = first % 4, second % 4
        y = jnp.where(self.c == 0, second, first)
        x = jnp.where(self.c == 0, first, second)
        return ((2 * y + x // 2 - self.z) % NZ) * 2 + x % 2


FROM = (0, 2, -1, 1)


def spread(block, first):
    return [block] + [plane_shift(block, first, amount) for amount in (2, 1, -1)]


def gather_tokens(out_grad, place):
    stack = jnp.stack(spread(out_grad, True))
    own = jnp.zeros((16, *out_grad.shape), BF)
    for second, piece in zip(FROM, spread(stack, False)):
        for k, first in enumerate(FROM):
            at = place.block(place.first + first, place.second + second)
            own = lax.dynamic_update_slice_in_dim(own, piece[k : k + 1], at, 0)
    return own


def hadamard_kernel(in_ref, out_ref):
    count, _, columns = in_ref.shape
    scale = 1.0 / math.sqrt(2 * count)

    def tile(i, carry):
        across = pl.ds(pl.multiple_of(i * 128, 128), 128)
        values = [in_ref[t, :, across].astype(F32) for t in range(count)]
        level = 1
        while level < count:
            values = [
                values[t] + values[t | level] if not t & level else values[t ^ level] - values[t]
                for t in range(count)
            ]
            level *= 2
        for t in range(count):
            out_ref[t, :, across] = values[t] * scale
        return carry

    lax.fori_loop(0, columns // 128, tile, 0)


def hadamard(values):
    return pl.pallas_call(
        hadamard_kernel,
        out_shape=jax.ShapeDtypeStruct(values.shape, F32),
        in_specs=[pl.BlockSpec(memory_space=pltpu.VMEM)],
        out_specs=pl.BlockSpec(memory_space=pltpu.VMEM),
        cost_estimate=pl.CostEstimate(flops=5 * values.size, bytes_accessed=8 * values.size, transcendentals=0),
    )(values)


def gates_kernel(core_ref, hidden_ref, gate_ref, up_ref, out_ref):
    half = hidden_ref.shape[0] // 2
    for low in range(2):
        hidden = hidden_ref[pl.ds(low * half, half)].reshape(64, -1)
        source = pl.ds(pl.multiple_of(low * 128 + core_ref[0] * 64, 64), 64)
        target = pl.ds(low * 64, 64)
        gate = gate_ref[source, :].astype(F32)
        upper = up_ref[source, :].astype(F32)
        logistic = 1.0 / (1.0 + jnp.exp(-gate))
        out_ref[0, target, :] = (hidden * upper * logistic * (1.0 + gate * (1.0 - logistic))).astype(BF)
        out_ref[1, target, :] = (hidden * gate * logistic).astype(BF)


def gates(core, hidden, gate, upper):
    size = hidden.size
    return pl.pallas_call(
        gates_kernel,
        out_shape=jax.ShapeDtypeStruct((2, 128, hidden.shape[-1]), BF),
        in_specs=[pl.BlockSpec(memory_space=pltpu.SMEM)] + [pl.BlockSpec(memory_space=pltpu.VMEM)] * 3,
        out_specs=pl.BlockSpec(memory_space=pltpu.VMEM),
        cost_estimate=pl.CostEstimate(flops=12 * size, bytes_accessed=12 * size, transcendentals=size),
    )(core.reshape(1), hidden, gate, upper)


def scatter_sum(own, other):
    def chain(direction):
        def rows(offset):
            return [side[direction * offset % NZ] for side in (own, other)]

        def hop(total):
            return ring(total.astype(BF), direction).astype(F32)

        side = 0 if direction == 1 else 1
        parts = rows(3)
        parts[side] = parts[side] + hop(rows(4)[side])
        total = jnp.stack(parts)
        for offset in (2, 1):
            total = jnp.stack(rows(offset)) + hop(total)
        return hop(total)

    right, left = chain(1), chain(-1)
    return own[0] + right[0] + left[0], other[0] + right[1] + left[1]


def mix(own, other, place):
    theirs = core_swap(other)
    total = own + theirs
    difference = jnp.where(place.c == 0, own - theirs, theirs - own)
    difference, total = (
        jnp.where(place.c == 0, difference, total),
        jnp.where(place.c == 0, total, difference),
    )
    rows = jnp.stack([total.reshape(16, 8, -1), difference.reshape(16, 8, -1)], axis=1)
    there = lax.all_to_all(rows.astype(BF).reshape(16, 16, -1), ("y", "x"), 0, 0)
    back = lax.all_to_all(hadamard(there), ("y", "x"), 0, 0).reshape(rows.shape)
    return back[:, 0], core_swap(back[:, 1])


def step(out_grad, gate_act, up_act, gate_weight, up_weight, down_weight):
    place = Place()
    width = out_grad.shape[1]
    tokens = gather_tokens(out_grad, place)
    other_tokens = core_swap(tokens)

    def partials(rows):
        return contract_rows(rows.reshape(-1, width), down_weight).reshape(NZ, 128, -1)

    own, other = scatter_sum(partials(tokens), partials(other_tokens))
    own, other = mix(own, other, place)
    own = gates(place.c, own, gate_act, up_act)
    other = gates(1 - place.c, other, gate_act, up_act)

    def back(part, dtype):
        right = left = part
        result = lax.optimization_barrier(jnp.zeros((NZ, 128, width), dtype))

        def product(gate, upper):
            rows = contract_rows(gate, gate_weight) + contract_rows(upper, up_weight)
            return rows.astype(dtype)

        def move(way, value):
            return ring(value, 1 if way == "r" else -1)

        result = result.at[0].set(product(part[0], part[1]))
        for step in (1, 2, 3):
            right, left = move("r", right), move("l", left)
            pair = [jnp.concatenate([right[i], left[i]], axis=0) for i in range(2)]
            rows = product(*pair)
            result = result.at[NZ - step].set(rows[:128]).at[step].set(rows[128:])
        return result, product(move("r", right[0]), move("l", left[1]))

    early, last = back(other, F32)
    early = core_swap(early)
    last = core_swap(last)
    arrived = early.at[4].set(last).reshape(16, 64, width)
    keep, last = back(own, F32)
    keep = keep.at[4].set(last).reshape(16, 64, width)

    def message(distance):
        def at(k):
            index = place.block(place.first + distance, jnp.int32(k))
            return (
                lax.dynamic_slice_in_dim(keep, index, 1, 0)
                + lax.dynamic_slice_in_dim(arrived, index, 1, 0).astype(F32)
            )

        return jnp.concatenate([at(k) for k in range(4)], axis=0)

    total = message(0)
    for distance in (2, 1, -1):
        total += plane_shift(message(distance).astype(BF), True, distance).astype(F32)

    def row(distance):
        return lax.dynamic_index_in_dim(total, (place.second + distance) % 4, 0, keepdims=False)

    result = row(0)
    for distance in (2, 1, -1):
        result += plane_shift(row(distance).astype(BF), False, distance).astype(F32)
    return result.astype(BF)


def solution(mesh):
    fine = Mesh(mesh.devices.reshape(NZ, NY, NX, NC), ("tok", *HID))
    rows, columns = P(HID, "tok"), P("tok", HID)
    in_specs = (rows, columns, columns, columns, columns, rows)
    return jax.shard_map(step, mesh=fine, in_specs=in_specs, out_specs=rows, check_vma=False)
```
